32 devices in a mesh: tok: 4 (over x, core), head: 4 (over z), seq: 2 (over y).
Axes of the slice: x: 2, y: 2, z: 4, core: 2. Of those that a mesh axis runs over, the one named last changes fastest.
Arguments:
- queries: bfloat16 [2, 4096, 2048], P('seq', ('tok', 'head')), may hold values from -6 to 6
- keys: bfloat16 [2, 4096, 2048], P('seq', ('tok', 'head')), may hold values from -6 to 6
- values: bfloat16 [2, 4096, 2048], P('seq', ('tok', 'head')), may hold values from -6 to 6
- rates: float32 [2, 4, 4096], P('seq', 'head', 'tok'), may hold values from 0.00015625 to 0.0015625
- fast_one: float32 [4, 512, 512], P('head'), may hold values from -0.25 to 0.25
- fast_two: float32 [4, 512, 512], P('head'), may hold values from -0.25 to 0.25
- fast_three: float32 [4, 512, 512], P('head'), may hold values from -0.25 to 0.25
- grad_out: bfloat16 [2, 4096, 2048], P('seq', ('tok', 'head')), may hold values from -6 to 6
Outputs:
- grad_queries: bfloat16 [2, 4096, 2048], P('seq', ('tok', 'head'))
- grad_keys: bfloat16 [2, 4096, 2048], P('seq', ('tok', 'head'))
- grad_values: bfloat16 [2, 4096, 2048], P('seq', ('tok', 'head'))
- grad_rates: float32 [2, 4, 4096], P('seq', 'head', 'tok')
- grad_fast_one: float32 [4, 512, 512], P('head')
- grad_fast_two: float32 [4, 512, 512], P('head')
- grad_fast_three: float32 [4, 512, 512], P('head')
The draws below stay inside these ranges and needn't reach their ends.
All inputs are finite; a program needn't handle non-finite values.
Results may differ from the reference program's by a relative error of at most 0.016.
Values may be sent and summed in bfloat16 or wider, within the bound.
No kernel may reach another device: no remote copies, remote signals or barrier semaphores. Data moves between devices by JAX's collectives and lax.ppermute only.
A program may use at most 128 MiB of HBM per device.

```python
import math
import jax
import jax.numpy as jnp
from jax import lax

P_SIZE = 512
F = 512
HEADS = 4
D = 2048
SEQS = 2
LENGTH = 4096


def block_levels(stream_key, extent, pieces, low, high):
    factor_of = 1.0
    for position, blocks in pieces:
        steps = jax.random.uniform(jax.random.fold_in(jax.random.fold_in(stream_key, 6), position), (blocks,), jnp.float32, low / len(pieces), high / len(pieces))
        factor_of = factor_of * jnp.repeat(jnp.exp(steps), extent[position] // blocks).reshape((-1,) + (1,) * (len(extent) - 1 - position))
    return factor_of


def scatter_about(key, extent, deviation, limit, cuts=(), kind=jnp.bfloat16):
    array = deviation * jax.random.normal(key, extent, jnp.float32)
    if cuts:
        array = array * block_levels(key, extent, cuts, -0.22, 0.18)
    return jnp.clip(array, -limit, limit).astype(kind)


def setup_inputs(seed: int = 0) -> dict:
    arg_keys = jax.random.split(jax.random.key(seed), 9)
    return {
        "queries": scatter_about(arg_keys[0], (SEQS, LENGTH, D), 1.0, 6.0, ((0, 2), (1, 16))),
        "keys": scatter_about(arg_keys[1], (SEQS, LENGTH, D), 1.0, 6.0, ((0, 2), (1, 16))),
        "values": scatter_about(arg_keys[2], (SEQS, LENGTH, D), 1.0, 6.0, ((0, 2), (1, 16))),
        "rates": jnp.clip(jnp.exp(math.log(0.0015625) - 2.3025851 * jax.random.uniform(arg_keys[3], (SEQS, HEADS, LENGTH), jnp.float32) ** block_levels(arg_keys[3], (SEQS, HEADS, LENGTH), ((0, 2), (1, 4), (2, 4)), -0.2, 0.2)), 0.00015625, 0.0015625),
        "fast_one": scatter_about(arg_keys[4], (HEADS, P_SIZE, F), P_SIZE ** -0.5, 0.25, ((0, 4),), jnp.float32),
        "fast_two": scatter_about(arg_keys[5], (HEADS, F, P_SIZE), F ** -0.5, 0.25, ((0, 4),), jnp.float32),
        "fast_three": scatter_about(arg_keys[6], (HEADS, P_SIZE, F), P_SIZE ** -0.5, 0.25, ((0, 4),), jnp.float32),
        "grad_out": scatter_about(arg_keys[7], (SEQS, LENGTH, D), 1.0, 6.0, ((0, 2), (1, 16))),
    }


epsilon = 1e-06

def matmul(left, right):
    return jnp.dot(left.astype(jnp.bfloat16), right.astype(jnp.bfloat16), preferred_element_type=jnp.float32)

def matmul_tn(left, right):
    return lax.dot_general(left.astype(jnp.bfloat16), right.astype(jnp.bfloat16), (((0,), (0,)), ((), ())), preferred_element_type=jnp.float32)

def matmul_nt(left, right):
    return lax.dot_general(left.astype(jnp.bfloat16), right.astype(jnp.bfloat16), (((1,), (1,)), ((), ())), preferred_element_type=jnp.float32)

def activation(preact):
    squash = jax.nn.sigmoid(preact)
    swished = preact * squash
    slope_one = squash * (1.0 + preact * (1.0 - squash))
    slope_two = squash * (1.0 - squash) * (2.0 + preact * (1.0 - 2.0 * squash))
    return (squash, swished, slope_one, slope_two)

def inner_forward(keys_h, values_h, rate_h, w_one, w_two, w_three):
    pre_one = matmul(keys_h, w_one)
    pre_three = matmul(keys_h, w_three)
    parts = activation(pre_one)
    swished, slope_one = (parts[1], parts[2])
    hidden = swished * pre_three
    target = -rate_h[:, None] * values_h.astype(jnp.float32)
    grad_two = matmul_tn(hidden, target)
    back_hidden = matmul_nt(target, w_two)
    delta_one = back_hidden * pre_three * slope_one
    delta_three = back_hidden * swished
    grad_one = matmul_tn(keys_h, delta_one)
    grad_three = matmul_tn(keys_h, delta_three)
    saved = (pre_one, pre_three, target, back_hidden, delta_one, delta_three)
    return ((grad_one, grad_two, grad_three), saved)

def normalize(weight, update):
    ref_norm = jnp.sqrt(lax.optimization_barrier(jnp.sum(weight * weight, axis=-2, keepdims=True)) + epsilon)
    upd_norm = jnp.sqrt(lax.optimization_barrier(jnp.sum(update * update, axis=-2, keepdims=True)) + epsilon)
    return (update * (ref_norm / upd_norm), ref_norm, upd_norm)

def apply_backward(queries_h, cotangent, new_one, new_two, new_three):
    pre_one = matmul(queries_h, new_one)
    pre_three = matmul(queries_h, new_three)
    parts = activation(pre_one)
    swished, slope_one = (parts[1], parts[2])
    hidden = swished * pre_three
    grad_two = matmul_tn(hidden, cotangent)
    back_hidden = matmul_nt(cotangent, new_two)
    delta_one = back_hidden * pre_three * slope_one
    delta_three = back_hidden * swished
    grad_one = matmul_tn(queries_h, delta_one)
    grad_three = matmul_tn(queries_h, delta_three)
    grad_queries = matmul_nt(delta_one, new_one) + matmul_nt(delta_three, new_three)
    return ((grad_one, grad_two, grad_three), grad_queries)

def adjoint(weight, update, ref_norm, upd_norm, grad_new):
    moment = lax.optimization_barrier(jnp.sum(grad_new * update, axis=-2, keepdims=True))
    factor = ref_norm / upd_norm
    grad_update = factor * grad_new - update * (factor * moment / (upd_norm * upd_norm))
    direct = weight * (moment / (upd_norm * ref_norm)) + grad_update
    return (-grad_update, direct)

def double_backward(keys_h, values_h, rate_h, w_one, w_two, w_three, saved, cot_one, cot_two, cot_three):
    pre_one, pre_three, target, back_hidden, delta_one, delta_three = saved
    parts = activation(pre_one)
    swished, slope_one, slope_two = (parts[1], parts[2], parts[3])
    hidden = swished * pre_three
    grad_hidden = matmul_nt(target, cot_two)
    grad_target = matmul(hidden, cot_two)
    grad_delta_one = matmul(keys_h, cot_one)
    grad_delta_three = matmul(keys_h, cot_three)
    grad_keys = matmul_nt(delta_one, cot_one) + matmul_nt(delta_three, cot_three)
    grad_back = grad_delta_one * pre_three * slope_one + grad_delta_three * swished
    grad_pre_three = grad_delta_one * back_hidden * slope_one + grad_hidden * swished
    grad_pre_one = grad_delta_one * back_hidden * pre_three * slope_two + grad_delta_three * back_hidden * slope_one + grad_hidden * pre_three * slope_one
    grad_target = grad_target + matmul(grad_back, w_two)
    weight_two = matmul_tn(grad_back, target)
    grad_keys = grad_keys + (matmul_nt(grad_pre_one, w_one) + matmul_nt(grad_pre_three, w_three))
    weight_one = matmul_tn(keys_h, grad_pre_one)
    weight_three = matmul_tn(keys_h, grad_pre_three)
    grad_values = -rate_h[:, None] * grad_target
    grad_rate = -lax.optimization_barrier(jnp.sum(values_h.astype(jnp.float32) * grad_target, axis=1))
    return (grad_keys, grad_values, grad_rate, (weight_one, weight_two, weight_three))

def reference(queries, keys, values, rates, fast_one, fast_two, fast_three, grad_out):
    width = fast_one.shape[1]
    query_rows, key_rows, value_rows, rate_rows = ([], [], [], [])
    totals = [[jnp.zeros_like(fast_one[0]), jnp.zeros_like(fast_two[0]), jnp.zeros_like(fast_three[0])] for head_idx in range(HEADS)]
    for seq_idx in range(SEQS):
        query_heads, key_heads, value_heads, rate_heads = ([], [], [], [])
        for head_idx in range(HEADS):
            start = head_idx * width
            keys_h = keys[seq_idx, :, start:start + width]
            values_h = values[seq_idx, :, start:start + width]
            queries_h = queries[seq_idx, :, start:start + width]
            cotangent = grad_out[seq_idx, :, start:start + width]
            rate_h = rates[seq_idx, head_idx]
            weights = (fast_one[head_idx], fast_two[head_idx], fast_three[head_idx])
            inner, saved = inner_forward(keys_h, values_h, rate_h, weights[0], weights[1], weights[2])
            normed = [normalize(weights[index], weights[index] - inner[index]) for index in range(3)]
            grads_new, grad_queries = apply_backward(queries_h, cotangent, normed[0][0], normed[1][0], normed[2][0])
            adjoints = [adjoint(weights[index], weights[index] - inner[index], normed[index][1], normed[index][2], grads_new[index]) for index in range(3)]
            grad_keys, grad_values, grad_rate, extra = double_backward(keys_h, values_h, rate_h, weights[0], weights[1], weights[2], saved, adjoints[0][0], adjoints[1][0], adjoints[2][0])
            for index in range(3):
                totals[head_idx][index] = totals[head_idx][index] + (adjoints[index][1] + extra[index])
            query_heads.append(grad_queries.astype(jnp.bfloat16))
            key_heads.append(grad_keys.astype(jnp.bfloat16))
            value_heads.append(grad_values.astype(jnp.bfloat16))
            rate_heads.append(grad_rate)
        query_rows.append(jnp.concatenate(query_heads, axis=1))
        key_rows.append(jnp.concatenate(key_heads, axis=1))
        value_rows.append(jnp.concatenate(value_heads, axis=1))
        rate_rows.append(jnp.stack(rate_heads))
    grad_fast_one = jnp.stack([totals[head_idx][0] for head_idx in range(HEADS)])
    grad_fast_two = jnp.stack([totals[head_idx][1] for head_idx in range(HEADS)])
    grad_fast_three = jnp.stack([totals[head_idx][2] for head_idx in range(HEADS)])
    return (jnp.stack(query_rows), jnp.stack(key_rows), jnp.stack(value_rows), jnp.stack(rate_rows), grad_fast_one, grad_fast_two, grad_fast_three)
```

```python
import functools

import jax
import jax.numpy as jnp
from jax import lax
from jax.experimental import pallas as pl
from jax.experimental.pallas import tpu as pltpu
from jax.sharding import PartitionSpec as P


epsilon = 1e-06
bf16 = jnp.bfloat16
f32 = jnp.float32


def dot_nn(left, right):
    return lax.dot_general(left, right, (((1,), (0,)), ((), ())), preferred_element_type=f32)


def dot_tn(left, right):
    return lax.dot_general(left, right, (((0,), (0,)), ((), ())), preferred_element_type=f32)


def dot_nt(left, right):
    return lax.dot_general(left, right, (((1,), (1,)), ((), ())), preferred_element_type=f32)


def sigmoid(x):
    return 0.5 * jnp.tanh(0.5 * x) + 0.5


def accumulate(acc, index, value, first):
    if first:
        acc[index] = value
    else:
        acc[index] += value


def emit_halves(idx, acc, keep, send):
    half = keep.shape[2]
    own = pl.multiple_of(idx[1] * half, half)
    other = pl.multiple_of((1 - idx[1]) * half, half)
    for j in range(3):
        keep[j] = acc[j, :, pl.ds(own, half)]
        send[j] = acc[j, :, pl.ds(other, half)].astype(bf16)


def join_halves(idx, own_ref, other_ref, out):
    half = own_ref.shape[2]
    own = pl.multiple_of(idx[1] * half, half)
    other = pl.multiple_of((1 - idx[1]) * half, half)
    for j in range(3):
        out[j, :, pl.ds(own, half)] = own_ref[j]
        out[j, :, pl.ds(other, half)] = other_ref[j]


def piece_rate(idx, rate, piece, rows):
    return rate[pl.ds(pl.multiple_of((idx[0] ^ piece) * rows, rows), rows), :]


def inner_kernel(count, idx, rate, w_one, w_two, w_three, *refs):
    keys, values = refs[:count], refs[count : 2 * count]
    keep, send, acc = refs[2 * count :]
    for p in range(count):
        k = keys[p][...]
        t = (-piece_rate(idx, rate, p, k.shape[0]) * values[p][...].astype(f32)).astype(bf16)
        a_one = dot_nn(k, w_one[...])
        a_three = dot_nn(k, w_three[...])
        b = dot_nt(t, w_two[...])
        sq = sigmoid(a_one)
        swished = a_one * sq
        slope = sq * (1.0 + a_one * (1.0 - sq))
        hidden = (swished * a_three).astype(bf16)
        d_one = (b * a_three * slope).astype(bf16)
        d_three = (b * swished).astype(bf16)
        accumulate(acc, 0, dot_tn(k, d_one), p == 0)
        accumulate(acc, 1, dot_tn(hidden, t), p == 0)
        accumulate(acc, 2, dot_tn(k, d_three), p == 0)
    emit_halves(idx, acc, keep, send)


def factor_kernel(count, idx, rate, w_one, w_two, w_three, *refs):
    keys, values = refs[:count], refs[count : 2 * count]
    key_o, value_o, hid_o, d_one_o, d_three_o, f_one, f_two, f_three, f_four = refs[2 * count :]
    for p in range(count):
        k = keys[p][...]
        v = values[p][...]
        t = (-piece_rate(idx, rate, p, k.shape[0]) * v.astype(f32)).astype(bf16)
        a_one = dot_nn(k, w_one[...])
        a_three = dot_nn(k, w_three[...])
        b = dot_nt(t, w_two[...])
        sq = sigmoid(a_one)
        swished = a_one * sq
        slope = sq * (1.0 + a_one * (1.0 - sq))
        slope_two = sq * (1.0 - sq) * (2.0 + a_one * (1.0 - 2.0 * sq))
        key_o[p] = k
        value_o[p] = v
        hid_o[p] = (swished * a_three).astype(bf16)
        d_one_o[p] = (b * a_three * slope).astype(bf16)
        d_three_o[p] = (b * swished).astype(bf16)
        f_one[p] = (a_three * slope).astype(bf16)
        f_two[p] = swished.astype(bf16)
        f_three[p] = (b * slope).astype(bf16)
        f_four[p] = (b * a_three * slope_two).astype(bf16)


def normalize_kernel(idx, mine, theirs, w_one, w_two, w_three, update, stats, new):
    half = mine.shape[2]
    own = pl.multiple_of(idx[1] * half, half)
    for j, weight in enumerate((w_one, w_two, w_three)):
        w = weight[:, pl.ds(own, half)]
        u = w - (mine[j].astype(f32) + theirs[j].astype(f32))
        ref_norm = jnp.sqrt(jnp.sum(w * w, axis=0, keepdims=True) + epsilon)
        upd_norm = jnp.sqrt(jnp.sum(u * u, axis=0, keepdims=True) + epsilon)
        update[j] = u
        stats[j, 0:1, :] = ref_norm
        stats[j, 1:2, :] = upd_norm
        new[j] = (u * (ref_norm / upd_norm)).astype(bf16)


def apply_kernel(count, idx, y_own, y_other, *refs):
    queries, cots = refs[:count], refs[count : 2 * count]
    grads = refs[2 * count : 3 * count]
    keep, send, y, acc = refs[3 * count :]
    join_halves(idx, y_own, y_other, y)
    for p in range(count):
        q = queries[p][...]
        e = cots[p][...]
        c_one = dot_nn(q, y[0])
        c_three = dot_nn(q, y[2])
        dm = dot_nt(e, y[1])
        sq = sigmoid(c_one)
        swished = c_one * sq
        slope = sq * (1.0 + c_one * (1.0 - sq))
        m = (swished * c_three).astype(bf16)
        d_one = (dm * c_three * slope).astype(bf16)
        d_three = (dm * swished).astype(bf16)
        accumulate(acc, 0, dot_tn(q, d_one), p == 0)
        accumulate(acc, 1, dot_tn(m, e), p == 0)
        accumulate(acc, 2, dot_tn(q, d_three), p == 0)
        grads[p][...] = (dot_nt(d_one, y[0]) + dot_nt(d_three, y[2])).astype(bf16)
    emit_halves(idx, acc, keep, send)


def adjoint_kernel(
    share, idx, mine, theirs, update, stats, w_one, w_two, w_three, cot, direct
):
    half = mine.shape[2]
    own = pl.multiple_of(idx[1] * half, half)
    for j, weight in enumerate((w_one, w_two, w_three)):
        w = weight[:, pl.ds(own, half)]
        u = update[j]
        ref_norm = stats[j, 0:1, :]
        upd_norm = stats[j, 1:2, :]
        dy = mine[j].astype(f32) + theirs[j].astype(f32)
        moment = jnp.sum(dy * u, axis=0, keepdims=True)
        factor = ref_norm / upd_norm
        du = factor * dy - u * (factor * moment / (upd_norm * upd_norm))
        cot[j] = (-du).astype(bf16)
        direct[j] = (w * (moment / (upd_norm * ref_norm)) + du) * share


def double_kernel(count, idx, rate, w_one, w_two, w_three, g_own, g_other, *refs):
    stacks = refs[:9]
    key_grads = refs[9 : 9 + count]
    value_grads = refs[9 + count : 9 + 2 * count]
    rate_grad, keep, send, g, acc = refs[9 + 2 * count :]
    p = pl.program_id(0)

    @pl.when(p == 0)
    def _():
        join_halves(idx, g_own, g_other, g)
        acc[...] = jnp.zeros_like(acc)

    k, v, hidden, d_one, d_three, f_one, f_two, f_three, f_four = [ref[0] for ref in stacks]
    rows = k.shape[0]
    r = piece_rate(idx, rate, p, rows)
    t = (-r * v.astype(f32)).astype(bf16)
    dh = dot_nt(t, g[1])
    dd_one = dot_nn(k, g[0])
    dd_three = dot_nn(k, g[2])
    f_one = f_one.astype(f32)
    f_two = f_two.astype(f32)
    f_three = f_three.astype(f32)
    f_four = f_four.astype(f32)
    db = (dd_one * f_one + dd_three * f_two).astype(bf16)
    da_three = (dd_one * f_three + dh * f_two).astype(bf16)
    da_one = (dd_one * f_four + dd_three * f_three + dh * f_one).astype(bf16)
    dt = dot_nn(hidden, g[1]) + dot_nn(db, w_two[...])
    acc[0] += dot_tn(k, da_one)
    acc[1] += dot_tn(db, t)
    acc[2] += dot_tn(k, da_three)
    gk = (
        (dot_nt(d_one, g[0]) + dot_nt(d_three, g[2]))
        + (dot_nt(da_one, w_one[...]) + dot_nt(da_three, w_three[...]))
    ).astype(bf16)
    gv = (-r * dt).astype(bf16)
    row = pl.multiple_of((idx[0] ^ p) * rows, rows)
    rate_grad[pl.ds(row, rows), :] = -jnp.sum(v.astype(f32) * dt, axis=1, keepdims=True)
    for i in range(count):

        @pl.when(p == i)
        def _():
            key_grads[i][...] = gk
            value_grads[i][...] = gv

    @pl.when(p == count - 1)
    def _():
        emit_halves(idx, acc, keep, send)


def join_kernel(idx, own_ref, other_ref, *outs):
    half = own_ref.shape[2]
    own = pl.multiple_of(idx[1] * half, half)
    other = pl.multiple_of((1 - idx[1]) * half, half)
    for j in range(3):
        outs[j][:, pl.ds(own, half)] = own_ref[j]
        outs[j][:, pl.ds(other, half)] = other_ref[j]


def call(kernel, name, operands, outs, scratch=(), **kwargs):
    smem = pl.BlockSpec(memory_space=pltpu.SMEM)
    vmem = pl.BlockSpec(memory_space=pltpu.VMEM)
    return pl.pallas_call(
        kernel,
        name=name,
        out_shape=outs,
        in_specs=[smem] + [vmem] * (len(operands) - 1),
        out_specs=[vmem] * len(outs),
        scratch_shapes=scratch,
        **kwargs,
    )(*operands)


def shape(dims, dtype):
    return jax.ShapeDtypeStruct(tuple(dims), dtype)


def xor_permute(x, axis, bit):
    size = lax.axis_size(axis)
    return lax.ppermute(x, axis, [(i, i ^ bit) for i in range(size)])


def body(queries, keys, values, rates, fast_one, fast_two, fast_three, grad_out):
    count = lax.axis_size("head")
    tok = lax.axis_size("tok")
    rows = keys.shape[1]
    fan_in, hidden_units = fast_one.shape[1], fast_one.shape[2]
    width = fan_in
    half = hidden_units // 2
    head = lax.axis_index("head").astype(jnp.int32)
    core = lax.axis_index("tok").astype(jnp.int32) & 1
    idx = jnp.stack([head, core])
    weights = (fast_one[0], fast_two[0], fast_three[0])
    low = tuple(w.astype(bf16) for w in weights)
    rate = rates.reshape(-1, 1)

    def cut(x):
        return [
            lax.dynamic_slice(x[0], (0, (head ^ p) * width), (rows, width)) for p in range(count)
        ]

    def exchange(pieces):
        return [pieces[0]] + [xor_permute(pieces[p], "head", p) for p in range(1, count)]

    def paste(pieces):
        out = jnp.zeros((rows, count * width), bf16)
        for p in range(count):
            out = lax.dynamic_update_slice(out, pieces[p], (0, (head ^ p) * width))
        return out[None]

    def tok_exchange(keep, sent):
        mine = (keep + sent.astype(f32)).astype(bf16)
        bit = 2
        theirs = xor_permute(mine, "tok", bit)
        while bit * 2 < tok:
            bit *= 2
            mine = (mine.astype(f32) + theirs.astype(f32)).astype(bf16)
            theirs = xor_permute(mine, "tok", bit)
        return mine, theirs

    block = (3, fan_in, half)
    halves = [shape(block, f32), shape(block, bf16)]
    square = (3, fan_in, hidden_units)

    key_cut, value_cut, query_cut, cot_cut = cut(keys), cut(values), cut(queries), cut(grad_out)
    key_p = exchange(key_cut)
    value_p = exchange(value_cut)
    key_p, value_p, query_cut, cot_cut = lax.optimization_barrier(
        (key_p, value_p, query_cut, cot_cut)
    )
    query_p = exchange(query_cut)
    cot_p = exchange(cot_cut)

    keep, send = call(
        functools.partial(inner_kernel, count),
        "inner",
        (idx, rate, *low, *key_p, *value_p),
        halves,
        [pltpu.VMEM(square, f32)],
    )
    idx_late, send = lax.optimization_barrier((idx, send))
    mine, theirs = tok_exchange(keep, xor_permute(send, "tok", 1))
    stack = shape((count, rows, width), bf16)
    stacks = call(
        functools.partial(factor_kernel, count),
        "factors",
        (idx_late, rate, *low, *key_p, *value_p),
        [stack] * 9,
    )
    update, stats, y_own = call(
        normalize_kernel,
        "normalize",
        (idx, mine, theirs, *weights),
        [shape(block, f32), shape((3, 2, half), f32), shape(block, bf16)],
    )
    y_other = xor_permute(y_own, "tok", 1)
    *grad_q, keep, send = call(
        functools.partial(apply_kernel, count),
        "apply",
        (idx, y_own, y_other, *query_p, *cot_p),
        [shape((rows, width), bf16)] * count + halves,
        [pltpu.VMEM(square, bf16), pltpu.VMEM(square, f32)],
    )
    mine, theirs = tok_exchange(keep, xor_permute(send, "tok", 1))
    query_back = paste(exchange(grad_q))
    cot_own, direct = call(
        functools.partial(adjoint_kernel, 2.0 / tok),
        "adjoint",
        (idx, mine, theirs, update, stats, *weights),
        [shape(block, bf16), shape(block, f32)],
    )
    cot_other = xor_permute(cot_own, "tok", 1)

    smem = pl.BlockSpec(memory_space=pltpu.SMEM)
    vmem = pl.BlockSpec(memory_space=pltpu.VMEM)
    pipe = pl.BlockSpec((1, rows, width), lambda p: (p, 0, 0))
    outs = (
        [shape((rows, width), bf16)] * (2 * count) + [shape((count * rows, 1), f32)] + halves
    )
    res = pl.pallas_call(
        functools.partial(double_kernel, count),
        name="double",
        grid=(count,),
        out_shape=outs,
        in_specs=[smem] + [vmem] * 6 + [pipe] * 9,
        out_specs=[vmem] * len(outs),
        scratch_shapes=[pltpu.VMEM(square, bf16), pltpu.VMEM(square, f32)],
    )(idx, rate, *low, cot_own, cot_other, *stacks)
    grad_k, grad_v = res[:count], res[count : 2 * count]
    rate_grad, keep, send = res[2 * count :]
    key_back = paste(exchange(grad_k))
    value_back = paste(exchange(grad_v))

    chip = (keep + direct) + xor_permute(send, "tok", 1).astype(f32)
    stages = [("tok", 1 << b) for b in range(1, tok.bit_length() - 1)]
    stages_seq = [("seq", 1 << b) for b in range(lax.axis_size("seq").bit_length() - 1)]
    cut_row = fan_in // 2
    parts = []
    for part, order in (
        (chip[:, :cut_row], stages + stages_seq),
        (chip[:, cut_row:], stages_seq + stages),
    ):
        for axis, bit in order:
            part = part.astype(bf16)
            part = part.astype(f32) + xor_permute(part, axis, bit).astype(f32)
        parts.append(part)
    total_own = jnp.concatenate(parts, axis=1)
    total_other = xor_permute(total_own, "tok", 1)
    totals = call(
        join_kernel,
        "join",
        (idx, total_own, total_other),
        [shape((fan_in, hidden_units), f32)] * 3,
    )
    rate_grads = rate_grad.reshape(rates.shape)
    return (query_back, key_back, value_back, rate_grads, *(t[None] for t in totals))


def solution(mesh):
    tokens = P("seq", ("tok", "head"), None)
    placed = (
        tokens,
        tokens,
        tokens,
        P("seq", "head", "tok"),
        P("head", None, None),
        P("head", None, None),
        P("head", None, None),
        tokens,
    )
    return jax.shard_map(
        body,
        mesh=mesh,
        in_specs=placed,
        out_specs=(
            tokens,
            tokens,
            tokens,
            P("seq", "head", "tok"),
            P("head", None, None),
            P("head", None, None),
            P("head", None, None),
        ),
        check_vma=False,
    )
```

```python
import functools

import jax
import jax.numpy as jnp
from jax import lax
from jax.experimental import pallas as pl
from jax.experimental.pallas import tpu as pltpu
from jax.sharding import PartitionSpec as P


epsilon = 1e-06
bf16 = jnp.bfloat16
f32 = jnp.float32


def dot_nn(left, right):
    return lax.dot_general(left, right, (((1,), (0,)), ((), ())), preferred_element_type=f32)


def dot_tn(left, right):
    return lax.dot_general(left, right, (((0,), (0,)), ((), ())), preferred_element_type=f32)


def dot_nt(left, right):
    return lax.dot_general(left, right, (((1,), (1,)), ((), ())), preferred_element_type=f32)


def sigmoid(x):
    return 0.5 * jnp.tanh(0.5 * x) + 0.5


def columns(idx, half):
    own = pl.multiple_of(idx[1] * half, half)
    other = pl.multiple_of((1 - idx[1]) * half, half)
    return own, other


def emit_halves(idx, pairs, keep, send):
    half = keep.shape[2]
    own, other = columns(idx, half)
    for j, (left, right) in enumerate(pairs):
        send[j] = dot_tn(left[...], right[:, pl.ds(other, half)]).astype(bf16)
    for j, (left, right) in enumerate(pairs):
        keep[j] = dot_tn(left[...], right[:, pl.ds(own, half)])


def join_halves(idx, own_ref, other_ref, out):
    half = own_ref.shape[2]
    own, other = columns(idx, half)
    for j in range(3):
        out[j, :, pl.ds(own, half)] = own_ref[j]
        out[j, :, pl.ds(other, half)] = other_ref[j]


def piece_rate(idx, rate, piece, rows):
    return rate[pl.ds(pl.multiple_of((idx[0] ^ piece) * rows, rows), rows), :]


def cut_kernel(idx, left, right, *outs):
    width = outs[0].shape[2]
    for p, out in enumerate(outs):
        lanes = pl.ds(pl.multiple_of((idx[0] ^ p) * width, width), width)
        out[0] = left[:, lanes]
        out[1] = right[:, lanes]


def inner_kernel(count, idx, rate, w_one, w_two, w_three, *refs):
    pieces = refs[:count]
    keep, send, kb, tb, hb, d_one_b, d_three_b = refs[count:]
    rows = pieces[0].shape[1]
    for p in range(count):
        at = slice(p * rows, (p + 1) * rows)
        k = pieces[p][0]
        t = (-piece_rate(idx, rate, p, rows) * pieces[p][1].astype(f32)).astype(bf16)
        a_one = dot_nn(k, w_one[...])
        a_three = dot_nn(k, w_three[...])
        b = dot_nt(t, w_two[...])
        sq = sigmoid(a_one)
        swished = a_one * sq
        slope = sq * (1.0 + a_one * (1.0 - sq))
        kb[at] = k
        tb[at] = t
        hb[at] = (swished * a_three).astype(bf16)
        d_one_b[at] = (b * a_three * slope).astype(bf16)
        d_three_b[at] = (b * swished).astype(bf16)
    emit_halves(idx, ((kb, d_one_b), (hb, tb), (kb, d_three_b)), keep, send)


def factor_kernel(count, idx, rate, w_one, w_two, w_three, *refs):
    pieces = refs[:count]
    key_o, value_o, hid_o, d_one_o, d_three_o, f_one, f_two, f_three, f_four = refs[count:]
    for p in range(count):
        k = pieces[p][0]
        v = pieces[p][1]
        t = (-piece_rate(idx, rate, p, k.shape[0]) * v.astype(f32)).astype(bf16)
        a_one = dot_nn(k, w_one[...])
        a_three = dot_nn(k, w_three[...])
        b = dot_nt(t, w_two[...])
        sq = sigmoid(a_one)
        swished = a_one * sq
        slope = sq * (1.0 + a_one * (1.0 - sq))
        slope_two = sq * (1.0 - sq) * (2.0 + a_one * (1.0 - 2.0 * sq))
        key_o[p] = k
        value_o[p] = v
        hid_o[p] = (swished * a_three).astype(bf16)
        d_one_o[p] = (b * a_three * slope).astype(bf16)
        d_three_o[p] = (b * swished).astype(bf16)
        f_one[p] = (a_three * slope).astype(bf16)
        f_two[p] = swished.astype(bf16)
        f_three[p] = (b * slope).astype(bf16)
        f_four[p] = (b * a_three * slope_two).astype(bf16)


def normalize_kernel(mine, theirs, weight, update, stats, new):
    w = weight[0]
    u = w - (mine[0].astype(f32) + theirs[0].astype(f32))
    ref_norm = jnp.sqrt(jnp.sum(w * w, axis=0, keepdims=True) + epsilon)
    upd_norm = jnp.sqrt(jnp.sum(u * u, axis=0, keepdims=True) + epsilon)
    update[0] = u
    stats[0, 0:1, :] = ref_norm
    stats[0, 1:2, :] = upd_norm
    new[0] = (u * (ref_norm / upd_norm)).astype(bf16)


def outer_piece(q, e, y, at, qb, eb, mb, d_one_b, d_three_b):
    c_one = dot_nn(q, y[0])
    c_three = dot_nn(q, y[2])
    dm = dot_nt(e, y[1])
    sq = sigmoid(c_one)
    swished = c_one * sq
    slope = sq * (1.0 + c_one * (1.0 - sq))
    qb[at] = q
    eb[at] = e
    mb[at] = (swished * c_three).astype(bf16)
    d_one_b[at] = (dm * c_three * slope).astype(bf16)
    d_three_b[at] = (dm * swished).astype(bf16)


def apply_early_kernel(count, idx, y_own, y_other, *refs):
    pieces = refs[:count]
    qb, eb, mb, d_one_b, d_three_b, y = refs[count:]
    join_halves(idx, y_own, y_other, y)
    rows = pieces[0].shape[1]
    for p in range(count):
        at = slice(p * rows, (p + 1) * rows)
        outer_piece(pieces[p][0], pieces[p][1], y, at, qb, eb, mb, d_one_b, d_three_b)


def apply_late_kernel(count, idx, y_own, y_other, *refs):
    pieces, early = refs[:count], refs[count : count + 5]
    keep, send, d_one_b, d_three_b, qb, eb, mb, y = refs[count + 5 :]
    join_halves(idx, y_own, y_other, y)
    rows = pieces[0].shape[1]
    start = early[0].shape[0]
    for source, target in zip(early, (qb, eb, mb, d_one_b, d_three_b)):
        target[:start] = source[...]
    for p in range(count):
        at = slice(start + p * rows, start + (p + 1) * rows)
        outer_piece(pieces[p][0], pieces[p][1], y, at, qb, eb, mb, d_one_b, d_three_b)
    emit_halves(idx, ((qb, d_one_b), (mb, eb), (qb, d_three_b)), keep, send)


def query_kernel(count, idx, y_own, y_other, d_one, d_three, *refs):
    grads, y = refs[:count], refs[count]
    join_halves(idx, y_own, y_other, y)
    rows = grads[0].shape[0]
    for p in range(count):
        at = slice(p * rows, (p + 1) * rows)
        grads[p][...] = (dot_nt(d_one[at], y[0]) + dot_nt(d_three[at], y[2])).astype(bf16)


def adjoint_kernel(mine, theirs, update, stats, cot, moments):
    u = update[0]
    ref_norm = stats[0, 0:1, :]
    upd_norm = stats[0, 1:2, :]
    dy = mine[0].astype(f32) + theirs[0].astype(f32)
    moment = jnp.sum(dy * u, axis=0, keepdims=True)
    factor = ref_norm / upd_norm
    cot[0] = (u * (factor * moment / (upd_norm * upd_norm)) - factor * dy).astype(bf16)
    moments[0] = moment


def double_kernel(base, count, idx, rate, w_one, w_two, w_three, g_own, g_other, *refs):
    stacks = refs[:9]
    grads = refs[9 : 9 + count]
    da_one_o, da_three_o, db_o, rate_grad, g = refs[9 + count :]
    step = pl.program_id(0)

    @pl.when(step == 0)
    def _():
        join_halves(idx, g_own, g_other, g)

    k, v, hidden, d_one, d_three, f_one, f_two, f_three, f_four = [ref[0] for ref in stacks]
    rows = k.shape[0]
    r = piece_rate(idx, rate, step + base, rows)
    v = v.astype(f32)
    t = (-r * v).astype(bf16)
    dd_one = dot_nn(k, g[0])
    dd_three = dot_nn(k, g[2])
    dh = dot_nt(t, g[1])
    f_one = f_one.astype(f32)
    f_two = f_two.astype(f32)
    f_three = f_three.astype(f32)
    f_four = f_four.astype(f32)
    db = (dd_one * f_one + dd_three * f_two).astype(bf16)
    da_three = (dd_one * f_three + dh * f_two).astype(bf16)
    da_one = (dd_one * f_four + dd_three * f_three + dh * f_one).astype(bf16)
    da_one_o[0] = da_one
    da_three_o[0] = da_three
    db_o[0] = db
    dt = dot_nn(hidden, g[1]) + dot_nn(db, w_two[...])
    gk = (
        (dot_nt(d_one, g[0]) + dot_nt(d_three, g[2]))
        + (dot_nt(da_one, w_one[...]) + dot_nt(da_three, w_three[...]))
    ).astype(bf16)
    gv = (-r * dt).astype(bf16)
    rate_grad[0] = -jnp.sum(v * dt, axis=1, keepdims=True)
    for i in range(count):

        @pl.when(step == i)
        def _():
            grads[i][0] = gk
            grads[i][1] = gv


def weights_kernel(count, idx, rate, keys, values, *refs):
    low, high = refs[:4], refs[4:8]
    keep, send, rate_out, kb, tb, a_one_b, a_three_b, bb = refs[8:]
    rows = keys.shape[1]
    split = low[0].shape[0]
    for p in range(count):
        at = slice(p * rows, (p + 1) * rows)
        source, s = (low, p) if p < split else (high, p - split)
        kb[at] = keys[p]
        tb[at] = (-piece_rate(idx, rate, p, rows) * values[p].astype(f32)).astype(bf16)
        a_one_b[at] = source[0][s]
        a_three_b[at] = source[1][s]
        bb[at] = source[2][s]
        rate_out[pl.ds(pl.multiple_of((idx[0] ^ p) * rows, rows), rows), :] = source[3][s]
    emit_halves(idx, ((kb, a_one_b), (bb, tb), (kb, a_three_b)), keep, send)


def join_kernel(idx, own_ref, other_ref, *outs):
    half = own_ref.shape[2]
    own, other = columns(idx, half)
    for j in range(3):
        outs[j][:, pl.ds(own, half)] = own_ref[j]
        outs[j][:, pl.ds(other, half)] = other_ref[j]


def call(kernel, operands, outs, scratch=()):
    smem = pl.BlockSpec(memory_space=pltpu.SMEM)
    vmem = pl.BlockSpec(memory_space=pltpu.VMEM)
    return pl.pallas_call(
        kernel,
        out_shape=outs,
        in_specs=[smem] + [vmem] * (len(operands) - 1),
        out_specs=[vmem] * len(outs),
        scratch_shapes=scratch,
    )(*operands)


def call_each(kernel, operands, outs):
    def spec(x):
        return pl.BlockSpec((1,) + x.shape[1:], lambda j: (j, 0, 0))

    return pl.pallas_call(
        kernel,
        grid=(3,),
        out_shape=outs,
        in_specs=[spec(x) for x in operands],
        out_specs=[spec(x) for x in outs],
    )(*operands)


def shape(dims, dtype):
    return jax.ShapeDtypeStruct(tuple(dims), dtype)


def xor_permute(x, axis, bit):
    size = lax.axis_size(axis)
    return lax.ppermute(x, axis, [(i, i ^ bit) for i in range(size)])


def body(queries, keys, values, rates, fast_one, fast_two, fast_three, grad_out):
    count = lax.axis_size("head")
    tok = lax.axis_size("tok")
    rows = keys.shape[1]
    fan_in, hidden_units = fast_one.shape[1], fast_one.shape[2]
    width = fan_in
    half = hidden_units // 2
    early = count // 2
    late = count - early
    head = lax.axis_index("head").astype(jnp.int32)
    core = lax.axis_index("tok").astype(jnp.int32) & 1
    idx = jnp.stack([head, core])
    weights = (fast_one[0], fast_two[0], fast_three[0])
    low = tuple(w.astype(bf16) for w in weights)
    weight_half = jnp.stack(
        [lax.dynamic_slice(w, (0, core * half), (fan_in, half)) for w in weights]
    )
    rate = rates.reshape(-1, 1)

    def exchange(pieces, first=1):
        return [
            piece if p == 0 else xor_permute(piece, "head", p)
            for p, piece in enumerate(pieces, first)
        ]

    def paste(pieces):
        out = jnp.zeros((rows, count * width), bf16)
        for p in reversed(range(count)):
            out = lax.dynamic_update_slice(out, pieces[p], (0, (head ^ p) * width))
        return out[None]

    def tok_exchange(keep, sent):
        mine = (keep + sent.astype(f32)).astype(bf16)
        bit = 2
        theirs = xor_permute(mine, "tok", bit)
        while bit * 2 < tok:
            bit *= 2
            mine = (mine.astype(f32) + theirs.astype(f32)).astype(bf16)
            theirs = xor_permute(mine, "tok", bit)
        return mine, theirs

    block = (3, fan_in, half)
    halves = [shape(block, f32), shape(block, bf16)]
    square = (3, fan_in, hidden_units)
    tokens = count * rows
    tall = (tokens, width)
    both = shape((2, rows, width), bf16)

    kv_cut = call(cut_kernel, (idx, keys[0], values[0]), [both] * count)
    qe_cut = call(cut_kernel, (idx, queries[0], grad_out[0]), [both] * count)
    kv = exchange(kv_cut, 0)
    qe = [qe_cut[0]]
    for p in range(1, count):
        kv[p], piece = lax.optimization_barrier((kv[p], qe_cut[p]))
        qe.append(xor_permute(piece, "head", p))

    keep, send = call(
        functools.partial(inner_kernel, count),
        (idx, rate, *low, *kv),
        halves,
        [pltpu.VMEM(tall, bf16)] * 5,
    )
    idx_late, send = lax.optimization_barrier((idx, send))
    mine, theirs = tok_exchange(keep, xor_permute(send, "tok", 1))
    stack = shape((count, rows, width), bf16)
    stacks = call(functools.partial(factor_kernel, count), (idx_late, rate, *low, *kv), [stack] * 9)
    update, stats, y_own = call_each(
        normalize_kernel,
        (mine, theirs, weight_half),
        [shape(block, f32), shape((3, 2, half), f32), shape(block, bf16)],
    )
    y_other = xor_permute(y_own, "tok", 1)
    begun = call(
        functools.partial(apply_early_kernel, early),
        (idx, y_own, y_other, *qe[:early]),
        [shape((early * rows, width), bf16)] * 5,
        [pltpu.VMEM(square, bf16)],
    )
    keep, send, d_one, d_three = call(
        functools.partial(apply_late_kernel, late),
        (idx, y_own, y_other, *qe[early:], *begun),
        halves + [shape(tall, bf16)] * 2,
        [pltpu.VMEM(tall, bf16)] * 3 + [pltpu.VMEM(square, bf16)],
    )
    mine, theirs = tok_exchange(keep, xor_permute(send, "tok", 1))
    grad_q = call(
        functools.partial(query_kernel, count),
        (idx, y_own, y_other, d_one, d_three),
        [shape((rows, width), bf16)] * count,
        [pltpu.VMEM(square, bf16)],
    )
    query_back = paste(exchange(grad_q, 0))
    cot_own, moment = call_each(
        adjoint_kernel,
        (mine, theirs, update, stats),
        [shape(block, bf16), shape((3, 1, half), f32)],
    )
    cot_other = xor_permute(cot_own, "tok", 1)

    def double(base, span):
        smem = pl.BlockSpec(memory_space=pltpu.SMEM)
        vmem = pl.BlockSpec(memory_space=pltpu.VMEM)
        read = pl.BlockSpec((1, rows, width), lambda p: (p + base, 0, 0))
        write = pl.BlockSpec((1, rows, width), lambda p: (p, 0, 0))
        column = pl.BlockSpec((1, rows, 1), lambda p: (p, 0, 0))
        res = pl.pallas_call(
            functools.partial(double_kernel, base, span),
            grid=(span,),
            out_shape=[both] * span
            + [shape((span, rows, width), bf16)] * 3
            + [shape((span, rows, 1), f32)],
            in_specs=[smem] + [vmem] * 6 + [read] * 9,
            out_specs=[vmem] * span + [write] * 3 + [column],
            scratch_shapes=[pltpu.VMEM(square, bf16)],
        )(idx, rate, *low, cot_own, cot_other, *stacks)
        return list(res[:span]), res[span:]

    grads_high, rest_high = double(early, late)
    grads_low, rest_low = double(0, early)
    kv_back = exchange(grads_low, 0) + exchange(grads_high, early)
    key_back = paste([piece[0] for piece in kv_back])
    value_back = paste([piece[1] for piece in kv_back])

    keep, send, rate_grad = call(
        functools.partial(weights_kernel, count),
        (idx, rate, *stacks[:2], *rest_low, *rest_high),
        halves + [shape((tokens, 1), f32)],
        [pltpu.VMEM(tall, bf16)] * 5,
    )
    ref_norm, upd_norm = stats[:, 0:1], stats[:, 1:2]
    factor = ref_norm / upd_norm
    direct = weight_half * (moment / (upd_norm * ref_norm)) + (
        factor * (mine.astype(f32) + theirs.astype(f32))
        - update * (factor * moment / (upd_norm * upd_norm))
    )
    chip = (keep + direct * (2.0 / tok)) + xor_permute(send, "tok", 1).astype(f32)
    stages = [("tok", 1 << b) for b in range(1, tok.bit_length() - 1)]
    stages_seq = [("seq", 1 << b) for b in range(lax.axis_size("seq").bit_length() - 1)]
    cut_row = fan_in // 2
    parts = []
    for part, order in (
        (chip[:, :cut_row], stages + stages_seq),
        (chip[:, cut_row:], stages_seq + stages),
    ):
        for axis, bit in order:
            part = part.astype(bf16)
            moved = xor_permute(part, axis, bit)
            part = part.astype(f32) + moved.astype(f32)
        parts.append(part)
    total_own = jnp.concatenate(parts, axis=1)
    total_other = xor_permute(total_own, "tok", 1)
    totals = call(
        join_kernel, (idx, total_own, total_other), [shape((fan_in, hidden_units), f32)] * 3
    )
    rate_grads = rate_grad.reshape(rates.shape)
    return (query_back, key_back, value_back, rate_grads, *(t[None] for t in totals))


def solution(mesh):
    tokens = P("seq", ("tok", "head"), None)
    placed = (
        tokens,
        tokens,
        tokens,
        P("seq", "head", "tok"),
        P("head", None, None),
        P("head", None, None),
        P("head", None, None),
        tokens,
    )
    return jax.shard_map(
        body,
        mesh=mesh,
        in_specs=placed,
        out_specs=(
            tokens,
            tokens,
            tokens,
            P("seq", "head", "tok"),
            P("head", None, None),
            P("head", None, None),
            P("head", None, None),
        ),
        check_vma=False,
    )
```

```python
import functools

import jax
import jax.numpy as jnp
from jax import lax
from jax.experimental import pallas as pl
from jax.experimental.pallas import tpu as pltpu
from jax.sharding import PartitionSpec as P


epsilon = 1e-06
bf16 = jnp.bfloat16
f32 = jnp.float32


def dot_nn(left, right):
    return lax.dot_general(left, right, (((1,), (0,)), ((), ())), preferred_element_type=f32)


def dot_nt(left, right):
    return lax.dot_general(left, right, (((1,), (1,)), ((), ())), preferred_element_type=f32)


def sigmoid(x):
    return 0.5 * jnp.tanh(0.5 * x) + 0.5


def columns(idx, half):
    own = pl.multiple_of(idx[1] * half, half)
    other = pl.multiple_of((1 - idx[1]) * half, half)
    return own, other


def emit_halves(idx, pairs, keep, send, extra=None):
    half = keep.shape[2]
    own, other = columns(idx, half)
    for j, (left, right) in enumerate(pairs):
        send[j] = dot_nn(left[...], right[:, pl.ds(other, half)]).astype(bf16)
    for j, (left, right) in enumerate(pairs):
        total = dot_nn(left[...], right[:, pl.ds(own, half)])
        keep[j] = total if extra is None else total + extra(j)


def join_halves(idx, own_ref, other_ref, out):
    half = own_ref.shape[2]
    own, other = columns(idx, half)
    for j in range(3):
        out[j, :, pl.ds(own, half)] = own_ref[j]
        out[j, :, pl.ds(other, half)] = other_ref[j]


def piece_rate(idx, rate, piece, rows):
    return rate[pl.ds(pl.multiple_of((idx[0] ^ piece) * rows, rows), rows), :]


def cut_kernel(idx, left, right, *outs):
    width = outs[0].shape[2]
    for p, out in enumerate(outs):
        lanes = pl.ds(pl.multiple_of((idx[0] ^ p) * width, width), width)
        out[0] = left[:, lanes]
        out[1] = right[:, lanes]


def inner_kernel(count, idx, rate, w_one, w_two, w_three, *refs):
    pieces = refs[:count]
    keep, send, kt, tb, ht, d_one_b, d_three_b = refs[count:]
    rows = pieces[0].shape[1]
    for p in range(count):
        at = slice(p * rows, (p + 1) * rows)
        k = pieces[p][0]
        t = (-piece_rate(idx, rate, p, rows) * pieces[p][1].astype(f32)).astype(bf16)
        a_one = dot_nn(k, w_one[...])
        a_three = dot_nn(k, w_three[...])
        b = dot_nt(t, w_two[...])
        sq = sigmoid(a_one)
        swished = a_one * sq
        slope = sq * (1.0 + a_one * (1.0 - sq))
        kt[:, at] = k.T
        tb[at] = t
        ht[:, at] = (swished * a_three).astype(bf16).T
        d_one_b[at] = (b * a_three * slope).astype(bf16)
        d_three_b[at] = (b * swished).astype(bf16)
    emit_halves(idx, ((kt, d_one_b), (ht, tb), (kt, d_three_b)), keep, send)


def factor_kernel(count, idx, rate, w_one, w_two, w_three, *refs):
    pieces = refs[:count]
    outs = refs[count : 2 * count]
    key_t, target_o = refs[2 * count :]
    for p in range(count):
        k = pieces[p][0]
        v = pieces[p][1]
        rows = k.shape[0]
        at = slice(p * rows, (p + 1) * rows)
        t = (-piece_rate(idx, rate, p, k.shape[0]) * v.astype(f32)).astype(bf16)
        a_one = dot_nn(k, w_one[...])
        a_three = dot_nn(k, w_three[...])
        b = dot_nt(t, w_two[...])
        sq = sigmoid(a_one)
        swished = a_one * sq
        slope = sq * (1.0 + a_one * (1.0 - sq))
        slope_two = sq * (1.0 - sq) * (2.0 + a_one * (1.0 - 2.0 * sq))
        key_t[:, at] = k.T
        target_o[at] = t
        kept = (
            k,
            v,
            swished * a_three,
            b * a_three * slope,
            b * swished,
            a_three * slope,
            swished,
            b * slope,
            b * a_three * slope_two,
        )
        for j, value in enumerate(kept):
            outs[p][j] = value.astype(bf16)


def normalize_kernel(idx, mine, theirs, weight, update, stats, new):
    for j in range(3):
        w = weight[j]
        u = w - (mine[j].astype(f32) + theirs[j].astype(f32))
        ref_norm = jnp.sqrt(jnp.sum(w * w, axis=0, keepdims=True) + epsilon)
        upd_norm = jnp.sqrt(jnp.sum(u * u, axis=0, keepdims=True) + epsilon)
        update[j] = u
        stats[j, 0:1, :] = ref_norm
        stats[j, 1:2, :] = upd_norm
        new[j] = (u * (ref_norm / upd_norm)).astype(bf16)


def outer_piece(q, e, y, at, qt, eb, mt, d_one_b, d_three_b):
    c_one = dot_nn(q, y[0])
    c_three = dot_nn(q, y[2])
    dm = dot_nt(e, y[1])
    sq = sigmoid(c_one)
    swished = c_one * sq
    slope = sq * (1.0 + c_one * (1.0 - sq))
    qt[:, at] = q.T
    eb[at] = e
    mt[:, at] = (swished * c_three).astype(bf16).T
    d_one_b[at] = (dm * c_three * slope).astype(bf16)
    d_three_b[at] = (dm * swished).astype(bf16)


def apply_early_kernel(count, idx, y_own, y_other, *refs):
    pieces = refs[:count]
    qt, eb, mt, d_one_b, d_three_b, y = refs[count:]
    join_halves(idx, y_own, y_other, y)
    rows = pieces[0].shape[1]
    for p in range(count):
        at = slice(p * rows, (p + 1) * rows)
        outer_piece(pieces[p][0], pieces[p][1], y, at, qt, eb, mt, d_one_b, d_three_b)


def apply_late_kernel(count, idx, y_own, y_other, *refs):
    pieces, early = refs[:count], refs[count : count + 5]
    keep, send, d_one_b, d_three_b, qt, eb, mt, y = refs[count + 5 :]
    join_halves(idx, y_own, y_other, y)
    rows = pieces[0].shape[1]
    start = early[1].shape[0]
    qt[:, :start] = early[0][...]
    mt[:, :start] = early[2][...]
    for j, target in ((1, eb), (3, d_one_b), (4, d_three_b)):
        target[:start] = early[j][...]
    for p in range(count):
        at = slice(start + p * rows, start + (p + 1) * rows)
        outer_piece(pieces[p][0], pieces[p][1], y, at, qt, eb, mt, d_one_b, d_three_b)
    emit_halves(idx, ((qt, d_one_b), (mt, eb), (qt, d_three_b)), keep, send)


def query_kernel(count, idx, y_own, y_other, d_one, d_three, *refs):
    grads, y = refs[:count], refs[count]
    join_halves(idx, y_own, y_other, y)
    rows = grads[0].shape[1]
    for p in range(count):
        at = slice(p * rows, (p + 1) * rows)
        grads[p][0] = (dot_nt(d_one[at], y[0]) + dot_nt(d_three[at], y[2])).astype(bf16)


def adjoint_kernel(idx, mine, theirs, update, stats, cot, moments):
    for j in range(3):
        u = update[j]
        ref_norm = stats[j, 0:1, :]
        upd_norm = stats[j, 1:2, :]
        dy = mine[j].astype(f32) + theirs[j].astype(f32)
        moment = jnp.sum(dy * u, axis=0, keepdims=True)
        factor = ref_norm / upd_norm
        cot[j] = (u * (factor * moment / (upd_norm * upd_norm)) - factor * dy).astype(bf16)
        moments[j] = moment


def adjoint_piece(r, kept, g):
    k = kept[0]
    t = (-r * kept[1].astype(f32)).astype(bf16)
    f_one, f_two, f_three, f_four = [kept[j].astype(f32) for j in range(5, 9)]
    dd_one = dot_nn(k, g[0])
    dd_three = dot_nn(k, g[2])
    dh = dot_nt(t, g[1])
    db = (dd_one * f_one + dd_three * f_two).astype(bf16)
    da_three = (dd_one * f_three + dh * f_two).astype(bf16)
    da_one = (dd_one * f_four + dd_three * f_three + dh * f_one).astype(bf16)
    return da_one, db, da_three


def input_piece(r, kept, g, weights, da_one, db, da_three, grad, rate_grad, p):
    w_one, w_two, w_three = weights
    dt = dot_nn(kept[2], g[1]) + dot_nn(db, w_two[...])
    grad[0] = (
        (dot_nt(kept[3], g[0]) + dot_nt(kept[4], g[2]))
        + (dot_nt(da_one, w_one[...]) + dot_nt(da_three, w_three[...]))
    ).astype(bf16)
    grad[1] = (-r * dt).astype(bf16)
    rate_grad[p] = -jnp.sum(kept[1].astype(f32) * dt, axis=1, keepdims=True)


def double_last_kernel(piece, idx, rate, w_one, w_two, w_three, g_own, g_other, *refs):
    kept, grad, rate_grad, da_one_o, db_o, da_three_o, g = refs
    join_halves(idx, g_own, g_other, g)
    rows = da_one_o.shape[0]
    r = piece_rate(idx, rate, piece, rows)
    da_one, db, da_three = adjoint_piece(r, kept, g)
    da_one_o[...] = da_one
    db_o[...] = db
    da_three_o[...] = da_three
    weights = (w_one, w_two, w_three)
    input_piece(r, kept, g, weights, da_one, db, da_three, grad, rate_grad, 0)


def double_inner_kernel(count, idx, rate, g_own, g_other, *refs):
    kept = refs[:count]
    da_one_o, db_o, da_three_o, g = refs[count:]
    join_halves(idx, g_own, g_other, g)
    rows = kept[0].shape[1]
    for p in range(count):
        at = slice(p * rows, (p + 1) * rows)
        r = piece_rate(idx, rate, p, rows)
        da_one_o[at], db_o[at], da_three_o[at] = adjoint_piece(r, kept[p], g)


def double_input_kernel(base, count, idx, rate, w_one, w_two, w_three, g_own, g_other, *refs):
    da_one, db, da_three = refs[:3]
    kept, grads = refs[3 : 3 + count], refs[3 + count : 3 + 2 * count]
    rate_grad, g = refs[3 + 2 * count :]
    join_halves(idx, g_own, g_other, g)
    rows = kept[0].shape[1]
    weights = (w_one, w_two, w_three)
    for p in range(count):
        at = slice((base + p) * rows, (base + p + 1) * rows)
        r = piece_rate(idx, rate, base + p, rows)
        input_piece(
            r, kept[p], g, weights, da_one[at], db[at], da_three[at], grads[p], rate_grad, p
        )


def weights_kernel(share, idx, key_t, target, *refs):
    mine, theirs, update, stats, moments, weight = refs[:6]
    first, last = refs[6:9], refs[9:12]
    keeps, sends = refs[12:14], refs[14:16]
    a_one_b, bt, a_three_b, direct = refs[16:]
    split = first[0].shape[0]
    for source, at in ((first, slice(0, split)), (last, slice(split, target.shape[0]))):
        a_one_b[at] = source[0][...]
        bt[:, at] = source[1][...].T
        a_three_b[at] = source[2][...]
    for j in range(3):
        ref_norm = stats[j, 0:1, :]
        upd_norm = stats[j, 1:2, :]
        moment = moments[j]
        factor = ref_norm / upd_norm
        dy = mine[j].astype(f32) + theirs[j].astype(f32)
        du = factor * dy - update[j] * (factor * moment / (upd_norm * upd_norm))
        direct[j] = (weight[j] * (moment / (upd_norm * ref_norm)) + du) * share
    half = weight.shape[2]
    rows = keeps[0].shape[1]
    own, other = columns(idx, half)
    pairs = ((key_t, a_one_b), (bt, target), (key_t, a_three_b))
    for j, (left, right) in enumerate(pairs):
        total = dot_nn(left[...], right[:, pl.ds(other, half)]).astype(bf16)
        sends[0][j] = total[:rows]
        sends[1][j] = total[rows:]
    for j, (left, right) in enumerate(pairs):
        total = dot_nn(left[...], right[:, pl.ds(own, half)]) + direct[j]
        keeps[0][j] = total[:rows]
        keeps[1][j] = total[rows:]


def join_kernel(count, idx, *refs):
    sides, outs = (refs[:count], refs[count : 2 * count]), refs[2 * count :]
    half = refs[0].shape[2]
    for lanes, parts in zip(columns(idx, half), sides):
        row = 0
        for part in parts:
            rows = part.shape[1]
            for j in range(3):
                outs[j][row : row + rows, pl.ds(lanes, half)] = part[j].astype(f32)
            row += rows


def paste_kernel(count, idx, *refs):
    pieces, outs = refs[:count], refs[count:]
    width = pieces[0].shape[-1]
    for p in range(count):
        lanes = pl.ds(pl.multiple_of((idx[0] ^ p) * width, width), width)
        for side, out in enumerate(outs):
            out[:, lanes] = pieces[p][side]


def call(kernel, operands, outs, scratch=()):
    smem = pl.BlockSpec(memory_space=pltpu.SMEM)
    vmem = pl.BlockSpec(memory_space=pltpu.VMEM)
    return pl.pallas_call(
        kernel,
        out_shape=outs,
        in_specs=[smem] + [vmem] * (len(operands) - 1),
        out_specs=[vmem] * len(outs),
        scratch_shapes=scratch,
    )(*operands)


def shape(dims, dtype):
    return jax.ShapeDtypeStruct(tuple(dims), dtype)


def xor_permute(x, axis, bit):
    size = lax.axis_size(axis)
    return lax.ppermute(x, axis, [(i, i ^ bit) for i in range(size)])


def body(queries, keys, values, rates, fast_one, fast_two, fast_three, grad_out):
    count = lax.axis_size("head")
    tok = lax.axis_size("tok")
    rows = keys.shape[1]
    fan_in, hidden_units = fast_one.shape[1], fast_one.shape[2]
    width = fan_in
    half = hidden_units // 2
    early = count // 2
    late = count - early
    head = lax.axis_index("head").astype(jnp.int32)
    core = lax.axis_index("tok").astype(jnp.int32) & 1
    idx = jnp.stack([head, core])
    weights = (fast_one[0], fast_two[0], fast_three[0])
    low = tuple(w.astype(bf16) for w in weights)
    weight_half = jnp.stack(
        [lax.dynamic_slice(w, (0, core * half), (fan_in, half)) for w in weights]
    )
    rate = rates.reshape(-1, 1)

    def exchange(pieces, first=1):
        return [
            piece if p == 0 else xor_permute(piece, "head", p)
            for p, piece in enumerate(pieces, first)
        ]

    def paste(pieces):
        out = shape((rows, count * width), bf16)
        sides = pieces[0].shape[0]
        kernel = functools.partial(paste_kernel, count)
        return [x[None] for x in call(kernel, (idx, *pieces), [out] * sides)]

    def tok_exchange(keep, sent):
        mine = (keep + sent.astype(f32)).astype(bf16)
        bit = 2
        theirs = xor_permute(mine, "tok", bit)
        while bit * 2 < tok:
            bit *= 2
            mine = (mine.astype(f32) + theirs.astype(f32)).astype(bf16)
            theirs = xor_permute(mine, "tok", bit)
        return mine, theirs

    block = (3, fan_in, half)
    halves = [shape(block, f32), shape(block, bf16)]
    square = (3, fan_in, hidden_units)
    tokens = count * rows
    tall = (tokens, width)
    flat = (width, tokens)
    both = shape((2, rows, width), bf16)

    kv_cut = call(cut_kernel, (idx, keys[0], values[0]), [both] * count)
    qe_cut = call(cut_kernel, (idx, queries[0], grad_out[0]), [both] * count)
    kv = exchange(kv_cut, 0)
    qe = [qe_cut[0]]
    for p in range(1, count):
        kv[p], piece = lax.optimization_barrier((kv[p], qe_cut[p]))
        qe.append(xor_permute(piece, "head", p))

    keep, send = call(
        functools.partial(inner_kernel, count),
        (idx, rate, *low, *kv),
        halves,
        [pltpu.VMEM(flat, bf16), pltpu.VMEM(tall, bf16)] * 2 + [pltpu.VMEM(tall, bf16)],
    )
    idx_late, send = lax.optimization_barrier((idx, send))
    mine, theirs = tok_exchange(keep, xor_permute(send, "tok", 1))
    stack = shape((9, rows, width), bf16)
    *kept, key_t, target = call(
        functools.partial(factor_kernel, count),
        (idx_late, rate, *low, *kv),
        [stack] * count + [shape(flat, bf16), shape(tall, bf16)],
    )
    update, stats, y_own = call(
        normalize_kernel,
        (idx, mine, theirs, weight_half),
        [shape(block, f32), shape((3, 2, half), f32), shape(block, bf16)],
    )
    y_other = xor_permute(y_own, "tok", 1)
    begun = call(
        functools.partial(apply_early_kernel, early),
        (idx, y_own, y_other, *qe[:early]),
        [shape((width, early * rows), bf16), shape((early * rows, width), bf16)] * 2
        + [shape((early * rows, width), bf16)],
        [pltpu.VMEM(square, bf16)],
    )
    keep, send, d_one, d_three = call(
        functools.partial(apply_late_kernel, late),
        (idx, y_own, y_other, *qe[early:], *begun),
        halves + [shape(tall, bf16)] * 2,
        [
            pltpu.VMEM(flat, bf16),
            pltpu.VMEM(tall, bf16),
            pltpu.VMEM(flat, bf16),
            pltpu.VMEM(square, bf16),
        ],
    )
    mine, theirs = tok_exchange(keep, xor_permute(send, "tok", 1))
    grad_q = call(
        functools.partial(query_kernel, count),
        (idx, y_own, y_other, d_one, d_three),
        [shape((1, rows, width), bf16)] * count,
        [pltpu.VMEM(square, bf16)],
    )
    (query_back,) = paste(exchange(grad_q, 0))
    cot_own, moment = call(
        adjoint_kernel,
        (idx, mine, theirs, update, stats),
        [shape(block, bf16), shape((3, 1, half), f32)],
    )
    cot_other = xor_permute(cot_own, "tok", 1)

    cots = (cot_own, cot_other)
    joined = [pltpu.VMEM(square, bf16)]
    final = count - 1
    grad, last_rate, *last = call(
        functools.partial(double_last_kernel, final),
        (idx, rate, *low, *cots, kept[final]),
        [both, shape((1, rows, 1), f32)] + [shape((rows, width), bf16)] * 3,
        joined,
    )
    kv_back = [None] * final + exchange([grad], final)
    inner_cots = call(
        functools.partial(double_inner_kernel, final),
        (idx, rate, *cots, *kept[:final]),
        [shape((final * rows, width), bf16)] * 3,
        joined,
    )
    cut_row = fan_in // 2
    part_block = (3, cut_row, half)
    results = call(
        functools.partial(weights_kernel, 2.0 / tok),
        (
            idx, key_t, target, mine, theirs, update, stats, moment, weight_half,
            *inner_cots, *last,
        ),
        [shape(part_block, f32)] * 2 + [shape(part_block, bf16)] * 2,
        [
            pltpu.VMEM(tall, bf16),
            pltpu.VMEM(flat, bf16),
            pltpu.VMEM(tall, bf16),
            pltpu.VMEM(block, f32),
        ],
    )
    rate_parts = [last_rate]
    for base, span in [(p, 1) for p in reversed(range(early, final))] + [(0, early)]:
        res = call(
            functools.partial(double_input_kernel, base, span),
            (idx, rate, *low, *cots, *inner_cots, *kept[base : base + span]),
            [both] * span + [shape((span, rows, 1), f32)],
            joined,
        )
        kv_back[base : base + span] = exchange(res[:span], base)
        rate_parts = [res[span], *rate_parts]
    key_back, value_back = paste(kv_back)
    rate_grad = jnp.concatenate(rate_parts, axis=0).reshape(count, rows)
    rate_grad = rate_grad[jnp.arange(count) ^ head]

    chips = [
        keep + xor_permute(send, "tok", 1).astype(f32)
        for keep, send in zip(results[:2], results[2:])
    ]
    stages = [("tok", 1 << b) for b in range(1, tok.bit_length() - 1)]
    stages_seq = [("seq", 1 << b) for b in range(lax.axis_size("seq").bit_length() - 1)]
    parts = []
    for part, order in ((chips[0], stages + stages_seq), (chips[1], stages_seq + stages)):
        for axis, bit in order:
            part = part.astype(bf16)
            moved = xor_permute(part, axis, bit)
            part = part.astype(f32) + moved.astype(f32)
        parts.append(part.astype(bf16))
    others = [xor_permute(x, "tok", 1) for x in parts]
    totals = call(
        functools.partial(join_kernel, len(parts)),
        (idx, *parts, *others),
        [shape((fan_in, hidden_units), f32)] * 3,
    )
    rate_grads = rate_grad.reshape(rates.shape)
    return (query_back, key_back, value_back, rate_grads, *(t[None] for t in totals))


def solution(mesh):
    tokens = P("seq", ("tok", "head"), None)
    placed = (
        tokens,
        tokens,
        tokens,
        P("seq", "head", "tok"),
        P("head", None, None),
        P("head", None, None),
        P("head", None, None),
        tokens,
    )
    return jax.shard_map(
        body,
        mesh=mesh,
        in_specs=placed,
        out_specs=(
            tokens,
            tokens,
            tokens,
            P("seq", "head", "tok"),
            P("head", None, None),
            P("head", None, None),
            P("head", None, None),
        ),
        check_vma=False,
    )
```
